32 devices in a mesh: ka: 8 (over z, y), row: 4 (over x, core).
Axes of the slice: x: 2, y: 2, z: 4, core: 2. Of those that a mesh axis runs over, the one named last changes fastest.
Arguments:
- occupied: bfloat16 [8, 8, 16384], P('ka', None, 'row'), may hold values from -6 to 6
- empty: bfloat16 [8, 64, 16384], P('ka', None, 'row'), may hold values from -6 to 6
- occ_energy: bfloat16 [8, 8], P('ka'), may hold values from -3 to -0.5
- emp_energy: bfloat16 [8, 64], P('ka'), may hold values from 0.5 to 3
- partner: int32 [2, 8], replicated, may hold values from 0 to 7, as said below
- gvecs: int32 [2, 384, 3], replicated, may hold values from -4 to 4
Outputs:
- polarity: float32 [2, 768, 768], P(None, 'ka', 'row')
The draws below stay inside these ranges and needn't reach their ends.
Inputs may be any that keep to these rules, and one draw needn't show every extreme that they name: partner[q, k] is the index of k + q_q on the periodic 4 x 2 x 1 grid of k-points, k = (i * 2 + j) + l, where each momentum q_q is a nonzero step along the first dimension only.
All inputs are finite; a program needn't handle non-finite values.
Results may differ from the reference program's by a relative error of at most 0.004.
Values may be sent and summed in bfloat16 or wider, within the bound.
No kernel may reach another device: no remote copies, remote signals or barrier semaphores. Data moves between devices by JAX's collectives and lax.ppermute only.
A program may use at most 64 MiB of HBM per device.

```python
import math
import jax
import jax.numpy as jnp
from jax import lax

NO = 8
NE = 64
NG = 384
Q = 2
GY = 16
GZ = 32
R = 16384
GX = 32
NK = 8
KX = 4
KY = 2
KZ = 1


def draw_partner(key, part):
    points = jnp.arange(NK, dtype=jnp.int32)
    point_x = points // (KY * KZ)
    rest = points % (KY * KZ)
    tables = []
    for moment in range(Q):
        subkey = jax.random.fold_in(key, 101 + moment)
        move_x = jax.random.randint(subkey, (), 1, KX).astype(jnp.int32)
        tables.append((point_x + move_x) % KX * (KY * KZ) + rest)
    return jnp.stack(tables).astype(jnp.int32)


def place_ends(values, key, least, largest):
    dims = values.shape
    place = [jax.random.randint(jax.random.fold_in(key, axis), (), 0, dims[axis]) for axis in range(len(dims))]
    values = values.at[tuple(place)].set(least)
    longest = dims.index(max(dims))
    place[longest] = (place[longest] + 1) % dims[longest]
    return values.at[tuple(place)].set(largest)


def shard_levels(rng, extent, shards, smallest, largest):
    def one(position, parts):
        heights = jax.random.uniform(jax.random.fold_in(jax.random.fold_in(rng, 6), position), (parts,), jnp.float32, smallest / len(shards), largest / len(shards))
        return jnp.repeat(jnp.exp(heights), extent[position] // parts).reshape((-1,) + (1,) * (len(extent) - position - 1))

    loudness = one(*shards[0])
    for cut in shards[1:]:
        loudness = loudness * one(*cut)
    return loudness


def scatter_about(stream_key, dims, width, reach, shards=(), held_as=jnp.bfloat16):
    factor_of = shard_levels(stream_key, dims, shards, -0.22, 0.18) if shards else 1.0
    entries = jax.random.normal(stream_key, dims, jnp.float32) * width * factor_of
    return jnp.minimum(jnp.maximum(entries, -reach), reach).astype(held_as)


def setup_inputs(seed: int = 0) -> dict:
    key_list = jax.random.split(jax.random.key(seed), 7)
    occupied = scatter_about(key_list[0], (NK, NO, R), 1.0, 6.0, ((0, 8), (2, 4)))
    empty = scatter_about(key_list[1], (NK, NE, R), 1.0, 6.0, ((0, 8), (2, 4)))
    occ_energy = jnp.clip(-3.0 + 2.5 * jax.random.uniform(key_list[2], (NK, NO), jnp.float32) ** shard_levels(key_list[2], (NK, NO), ((0, 8),), -0.2, 0.2), -3.0, -0.5).astype(jnp.bfloat16)
    emp_energy = jnp.clip(0.5 + 2.5 * jax.random.uniform(key_list[3], (NK, NE), jnp.float32) ** shard_levels(key_list[3], (NK, NE), ((0, 8),), -0.2, 0.2), 0.5, 3.0).astype(jnp.bfloat16)
    partner = draw_partner(jax.random.fold_in(key_list[6], 71), 0)
    gvecs = place_ends(jax.random.randint(key_list[5], (Q, NG, 3), -4, 5), jax.random.fold_in(key_list[5], 1), -4, 4).astype(jnp.int32)
    return dict(occupied=occupied, empty=empty, occ_energy=occ_energy, emp_energy=emp_energy, partner=partner, gvecs=gvecs)


def phase_table(plane_waves, start_point, point_count, grid_x, grid_y, grid_z):
    grid_total = grid_x * grid_y * grid_z
    points = start_point + lax.iota(jnp.int32, point_count)
    coord_z = points % grid_z
    coord_y = (points // grid_z) % grid_y
    coord_x = points // (grid_y * grid_z)
    phase_index = (plane_waves[:, 0:1] * coord_x[None, :] * (grid_y * grid_z)
                   + plane_waves[:, 1:2] * coord_y[None, :] * (grid_x * grid_z)
                   + plane_waves[:, 2:3] * coord_z[None, :] * (grid_x * grid_y)) % grid_total
    angle = phase_index.astype(jnp.float32) * (2.0 * math.pi / grid_total)
    return jnp.concatenate([jnp.cos(angle), jnp.sin(angle)], axis=0).astype(jnp.bfloat16)


def reference(occupied, empty, occ_energy, emp_energy, partner, gvecs):
    outputs = []
    for moment in range(Q):
        table_q = phase_table(gvecs[moment], 0, R, GX, GY, GZ)

        def accumulate(index, carry):
            source = partner[moment, index].astype(jnp.int32)
            occ_block = lax.dynamic_index_in_dim(occupied, index, 0, keepdims=False)
            emp_block = lax.dynamic_index_in_dim(empty, source, 0, keepdims=False)
            occ_level = lax.dynamic_index_in_dim(occ_energy, index, 0, keepdims=False)
            emp_level = lax.dynamic_index_in_dim(emp_energy, source, 0, keepdims=False)
            density = (occ_block.astype(jnp.float32)[:, None, :] * emp_block.astype(jnp.float32)[None, :, :]).reshape(NO * NE, R).astype(jnp.bfloat16)
            projected = lax.dot_general(density, table_q, (((1,), (1,)), ((), ())), preferred_element_type=jnp.float32) * (1.0 / R)
            weight = (1.0 / (emp_level.astype(jnp.float32)[None, :] - occ_level.astype(jnp.float32)[:, None])).reshape(NO * NE)
            left_side = projected.astype(jnp.bfloat16)
            right_side = (weight[:, None] * projected).astype(jnp.bfloat16)
            return carry + lax.dot_general(left_side, right_side, (((0,), (0,)), ((), ())), preferred_element_type=jnp.float32)

        outputs.append(lax.fori_loop(0, NK, accumulate, jnp.zeros((2 * NG, 2 * NG), jnp.float32)))
    return jnp.stack(outputs)
```

```python
import functools
import math

import jax
import jax.numpy as jnp
import numpy as np
from jax import lax
from jax.experimental import pallas as pl
from jax.experimental.pallas import tpu as pltpu
from jax.sharding import PartitionSpec as P

GY = 16
GZ = 32
REACH = 4
SHIFTS = 4
LANES = 128

SIDE = 2 * REACH + 1
FACTORS = SIDE
HALF = LANES // 2


def plane_table():
    u = np.arange(HALF)
    h1 = (u + REACH) // SIDE
    h2 = u - SIDE * h1
    y, z = np.divmod(np.arange(GY * GZ), GZ)
    turns = (h1[None, :] * y[:, None] * GZ + h2[None, :] * z[:, None] * GY) % (GY * GZ)
    angle = 2.0 * np.pi * turns / (GY * GZ)
    used = (u <= (SIDE * SIDE) // 2)[None, :]
    whole = np.concatenate([np.cos(angle) * used, np.sin(angle) * used], axis=1).astype(np.float32)
    high = whole.astype(jnp.bfloat16)
    low = (whole - high.astype(np.float32)).astype(jnp.bfloat16)
    return np.concatenate([high, low], axis=1)


def line_table(grid_x):
    x = np.arange(grid_x)
    rows = [np.cos(2.0 * np.pi * (g * x % grid_x) / grid_x) for g in range(REACH + 1)]
    rows += [np.sin(2.0 * np.pi * (g * x % grid_x) / grid_x) for g in range(1, REACH + 1)]
    return np.stack(rows).astype(np.float32)


def column_matrix(waves):
    g0, flat = waves[:, 0], waves[:, 1] * SIDE + waves[:, 2]
    u = jnp.abs(flat)
    turn = jnp.where(flat < 0, -1, 1)
    side = jnp.sign(g0)
    cos_row = jnp.abs(g0) * LANES + u
    cos_row2 = jnp.abs(g0) * LANES + HALF + u
    sin_at = jnp.where(g0 == 0, 0, REACH + jnp.abs(g0))
    sin_row = sin_at * LANES + u
    sin_row2 = sin_at * LANES + HALF + u
    half = waves.shape[0] // 2

    def order(cosine, sine):
        return jnp.concatenate([cosine[:half], sine[:half], cosine[half:], sine[half:]])

    one = order(jnp.ones_like(g0), side)
    two = order(-turn * side, turn)
    row_one = order(cos_row, sin_row)
    row_two = order(sin_row2, cos_row2)
    rows = lax.broadcasted_iota(jnp.int32, (FACTORS * LANES, 2 * waves.shape[0]), 0)
    matrix = jnp.where(rows == row_one[None, :], one[None, :], 0) + jnp.where(rows == row_two[None, :], two[None, :], 0)
    return matrix.astype(jnp.bfloat16)


def vmem(count):
    return [pl.BlockSpec(memory_space=pltpu.VMEM)] * count


SMEM = pl.BlockSpec(memory_space=pltpu.SMEM)


def add_block(row, line, emp, occ, plane, wide, density, part, total, first):
    bands = emp.shape[0]
    states = occ.shape[0]
    sheet = plane.shape[0]
    count = emp.shape[1] // sheet
    wide[...] = occ[...].astype(jnp.float32)
    for step in range(count):
        points = pl.ds(step * sheet, sheet)
        block = emp[:, points].astype(jnp.float32)
        for v in range(states):
            density[step, v * bands : (v + 1) * bands, :] = (wide[v : v + 1, points] * block).astype(jnp.bfloat16)
        made = jnp.dot(density[step], plane[...], preferred_element_type=jnp.float32)
        part[step] = made[:, :LANES] + made[:, LANES:]
    factor = [[line[j, row * count + step] for step in range(count)] for j in range(FACTORS)]
    tall = 16

    def fold(at, carry):
        rows = pl.ds(pl.multiple_of(at * tall, tall), tall)
        terms = [part[step, rows, :] for step in range(count)]
        for j in range(FACTORS):
            value = terms[0] * factor[j][0]
            for step in range(1, count):
                value = value + terms[step] * factor[j][step]
            if first:
                total[j, rows, :] = value
            else:
                total[j, rows, :] = total[j, rows, :] + value
        return carry

    lax.fori_loop(0, bands * states // tall, fold, 0)


def early_kernel(rows, line, e0, e1, e2, o0, o1, o2, plane, total, wide, density, part):
    for index, (emp, occ) in enumerate(((e0, o0), (e1, o1), (e2, o2))):
        add_block(rows[index], line, emp, occ, plane, wide, density, part, total, index == 0)


def late_kernel(scale, rows, line, e3, o3, plane, before, matrix, left, wide, density, part, total, narrow):
    total[...] = before[...]
    add_block(rows[3], line, e3, o3, plane, wide, density, part, total, False)
    for j in range(FACTORS):
        narrow[:, j * LANES : (j + 1) * LANES] = total[j].astype(jnp.bfloat16)
    proj = jnp.dot(narrow[...], matrix[...], preferred_element_type=jnp.float32)
    left[...] = (proj * scale).astype(jnp.bfloat16)


def project(blocks, rows, matrix, grid_x, scale):
    emps, occs = zip(*blocks)
    bands, points = emps[0].shape
    states = occs[0].shape[0]
    pairs = bands * states
    sheet = GY * GZ
    count = points // sheet
    plane = jnp.asarray(plane_table())
    line = jnp.asarray(line_table(grid_x))
    scratch = [
        pltpu.VMEM((states, points), jnp.float32),
        pltpu.VMEM((count, pairs, sheet), jnp.bfloat16),
        pltpu.VMEM((count, pairs, LANES), jnp.float32),
    ]
    total_shape = (FACTORS, pairs, LANES)
    total = pl.pallas_call(
        early_kernel,
        out_shape=jax.ShapeDtypeStruct(total_shape, jnp.float32),
        in_specs=[SMEM, SMEM] + vmem(7),
        out_specs=vmem(1)[0],
        scratch_shapes=scratch,
        name="early",
    )(rows, line, *emps[:3], *occs[:3], plane)
    return pl.pallas_call(
        functools.partial(late_kernel, scale),
        out_shape=jax.ShapeDtypeStruct((pairs, matrix.shape[1]), jnp.bfloat16),
        in_specs=[SMEM, SMEM] + vmem(5),
        out_specs=vmem(1)[0],
        scratch_shapes=scratch
        + [pltpu.VMEM(total_shape, jnp.float32), pltpu.VMEM((pairs, FACTORS * LANES), jnp.bfloat16)],
        name="late",
    )(rows, line, emps[3], occs[3], plane, total, matrix)


def gram_values(core, own, other, w_own, w_other, gram):
    width = own.shape[1] // 2
    at = pl.multiple_of(core * width, LANES)

    def product(values, weights):
        right = [
            (values[:, pl.ds(at + tile * LANES, LANES)].astype(jnp.float32) * weights[...]).astype(jnp.bfloat16)
            for tile in range(width // LANES)
        ]
        return lax.dot_general(
            values[...],
            jnp.concatenate(right, axis=1),
            (((0,), (0,)), ((), ())),
            preferred_element_type=jnp.float32,
        )

    gram[...] = product(own, w_own) + product(other, w_other)


def roll_half(value):
    return pltpu.roll(value, value.shape[1] // 2, 1)


def gram_kernel(place, own, other, w_own, w_other, keep, to_y, to_x, to_xy, gram):
    core, x, y = place[0], place[1], place[2]
    gram_values(core, own, other, w_own, w_other, gram)
    rows = gram.shape[0] // 8
    order = (0, 2, 1, 3)
    low = lax.broadcasted_iota(jnp.int32, (rows, gram.shape[1]), 1) < gram.shape[1] // 2

    def quadrant(way, zl):
        lower = gram[pl.ds(pl.multiple_of(order[zl] * 2 * rows + way * rows, 8), rows), :]
        upper = gram[pl.ds(pl.multiple_of(order[2 + zl] * 2 * rows + way * rows, 8), rows), :]
        return jnp.where(low, lower, roll_half(upper)), jnp.where(low, roll_half(lower), upper)

    for zl in range(2):
        at = slice(zl * rows, (zl + 1) * rows)
        for way, near, far in ((y, keep, to_x), (1 - y, to_y, to_xy)):
            zero, one = quadrant(way, zl)
            near[at, :] = jnp.where(x == 0, zero, one).astype(near.dtype)
            far[at, :] = jnp.where(x == 0, one, zero).astype(far.dtype)


def middle_kernel(place, keep, from_y, from_x, from_xy, stay, *refs):
    sends, block = refs[:3], refs[3]
    x, z = place[1], place[3]
    rows = keep.shape[0] // 2
    low = lax.broadcasted_iota(jnp.int32, (rows, keep.shape[1]), 1) < keep.shape[1] // 2
    for zl in range(2):
        at = slice(zl * rows, (zl + 1) * rows)
        same = keep[at, :] + from_y[at, :].astype(jnp.float32)
        cross = from_x[at, :].astype(jnp.float32) + from_xy[at, :].astype(jnp.float32)
        zero = jnp.where(x == 0, same, cross)
        one = jnp.where(x == 0, cross, same)
        block[zl] = jnp.where(low, zero, roll_half(one))
        block[2 + zl] = jnp.where(low, roll_half(zero), one)
    stay[...] = block[z]
    for index, send in enumerate(sends):
        send[...] = block[z ^ (index + 1)].astype(send.dtype)


def final_kernel(stay, one, two, three, out):
    total = stay[...] + one[...].astype(jnp.float32)
    total = total + two[...].astype(jnp.float32) + three[...].astype(jnp.float32)
    width = total.shape[1] // 2
    out[0] = total[:, :width]
    out[1] = roll_half(total)[:, :width]


def reduce_near(place, own, other, w_own, w_other):
    wide = own.shape[1]
    kcount, rcount = lax.axis_size("ka"), lax.axis_size("row")
    quarter = (wide // 4, wide // 2)
    keep, to_y, to_x, to_xy = pl.pallas_call(
        gram_kernel,
        out_shape=[jax.ShapeDtypeStruct(quarter, d) for d in (jnp.float32, jnp.bfloat16, jnp.bfloat16, jnp.bfloat16)],
        in_specs=[SMEM] + vmem(4),
        out_specs=vmem(4),
        scratch_shapes=[pltpu.VMEM((wide, wide // 2), jnp.float32)],
        name="gram",
    )(place, own, other, w_own, w_other)

    def route(dy, dx):
        return [(k * rcount + r, (k ^ dy) * rcount + (r ^ dx)) for k in range(kcount) for r in range(rcount)]

    both = ("ka", "row")
    from_y = lax.ppermute(to_y, both, route(1, 0))
    from_xy = lax.ppermute(to_xy, both, route(1, 2))
    from_x = lax.ppermute(to_x, both, route(0, 2))
    piece = (quarter[0] // 2, quarter[1])
    stay, *sends = pl.pallas_call(
        middle_kernel,
        out_shape=[jax.ShapeDtypeStruct(piece, jnp.float32)] + [jax.ShapeDtypeStruct(piece, jnp.bfloat16)] * 3,
        in_specs=[SMEM] + vmem(4),
        out_specs=vmem(4),
        scratch_shapes=[pltpu.VMEM((4,) + piece, jnp.float32)],
        name="middle",
    )(place, keep, from_y, from_x, from_xy)
    arrived = [lax.ppermute(send, both, route(2 * (m + 1), 0)) for m, send in enumerate(sends)]
    return pl.pallas_call(
        final_kernel,
        out_shape=jax.ShapeDtypeStruct((2, piece[0], piece[1] // 2), jnp.float32),
        in_specs=vmem(4),
        out_specs=vmem(1)[0],
        name="final",
    )(stay, *arrived)


def reduce_far(place, own, other, w_own, w_other):
    kcount = lax.axis_size("ka")
    wide = own.shape[1]
    width = wide // 4
    left = jnp.concatenate([own, other], axis=0)
    weight = jnp.concatenate([w_own[:, :1], w_other[:, :1]], axis=0)
    right = lax.dynamic_slice_in_dim(left, place[0] * 2 * width, 2 * width, 1)
    right = (right.astype(jnp.float32) * weight).astype(jnp.bfloat16)
    gram = lax.dot_general(left, right, (((0,), (0,)), ((), ())), preferred_element_type=jnp.float32)
    gram = gram.reshape(2, 2, width, 2, width).swapaxes(0, 1).reshape(kcount, wide // kcount, 2, width)
    parts = lax.all_to_all(gram.astype(jnp.bfloat16), "ka", 0, 0, tiled=True)
    total = jnp.sum(parts.astype(jnp.float32), axis=0)
    mine = lax.dynamic_index_in_dim(total, place[1], 1, keepdims=False)
    send = lax.dynamic_index_in_dim(total, 1 - place[1], 1, keepdims=False)
    came = lax.ppermute(send, "row", [(r, r ^ 2) for r in range(lax.axis_size("row"))])
    first = place[1] == 0
    return jnp.stack([jnp.where(first, mine, came), jnp.where(first, came, mine)])


def per_device(occupied, empty, occ_energy, emp_energy, partner, gvecs):
    kcount, rcount = lax.axis_size("ka"), lax.axis_size("row")
    assert rcount == 4 and partner.shape[0] == 2
    k, r = lax.axis_index("ka"), lax.axis_index("row")
    x, core = r // 2, r % 2
    points = occupied.shape[2]
    grid_x = points * rcount // (GY * GZ)
    emp = empty[0]
    half = emp.shape[0] // 2
    mine = lax.dynamic_slice_in_dim(emp, core * half, half, 0)
    theirs = lax.dynamic_slice_in_dim(emp, (1 - core) * half, half, 0)
    emp_x = lax.ppermute(mine, "row", [(i, i ^ 2) for i in range(rcount)])
    emp_xc = lax.ppermute(theirs, "row", [(i, i ^ 3) for i in range(rcount)])
    emp_c = lax.ppermute(theirs, "row", [(i, i ^ 1) for i in range(rcount)])

    stride = kcount // min(SHIFTS, kcount)
    choices = min(SHIFTS, kcount) - 1
    steps = jnp.clip(partner[:, 0] // stride, 1, choices) - 1

    def fetch(shift, operands):
        block, level = operands

        def route(dx):
            pairs = []
            for i in range(kcount):
                for j in range(rcount):
                    to = j ^ dx
                    pairs.append((i * rcount + j, (i + shift[to // 2] * stride) % kcount * rcount + to))
            return pairs

        both = ("ka", "row")
        return lax.ppermute(block, both, route(0)), lax.ppermute(block, both, route(2)), lax.ppermute(level, both, route(0))

    branches = [
        functools.partial(fetch, (one + 1, two + 1)) for one in range(choices) for two in range(choices)
    ]
    occ_own, occ_x, level = lax.switch(steps[0] * choices + steps[1], branches, (occupied[0], occ_energy))
    swap = [(i, i ^ 1) for i in range(rcount)]
    occ_c, occ_xc = lax.ppermute(occ_own, "row", swap), lax.ppermute(occ_x, "row", swap)

    matrix = column_matrix(lax.dynamic_index_in_dim(gvecs, x, 0, keepdims=False))
    rows = jnp.stack([r, r ^ 1, r ^ 2, r ^ 3]).astype(jnp.int32)
    place = jnp.stack([core, x, k % 2, k // 2]).astype(jnp.int32)
    left = project(
        ((mine, occ_own), (emp_c, occ_c), (emp_x, occ_x), (emp_xc, occ_xc)), rows, matrix, grid_x, 1.0 / (points * rcount)
    )
    states = occupied.shape[1]

    def weights(which):
        energy = lax.dynamic_slice_in_dim(emp_energy[0], which * half, half, 0).astype(jnp.float32)
        value = 1.0 / (energy[None, :] - level[0].astype(jnp.float32)[:, None])
        return jnp.broadcast_to(value.reshape(states * half, 1), (states * half, LANES))

    other = lax.ppermute(left, "row", swap)
    reduce = reduce_near if kcount == 8 else reduce_far
    return reduce(place, left, other, weights(core), weights(1 - core))


def solution(mesh):
    placed = (P("ka", None, "row"), P("ka", None, "row"), P("ka", None), P("ka", None), P(), P())
    return jax.shard_map(
        per_device, mesh=mesh, in_specs=placed, out_specs=P(None, "ka", "row"), check_vma=False
    )
```

```python
import functools
import math

import jax
import jax.numpy as jnp
import numpy as np
from jax import lax
from jax.experimental import pallas as pl
from jax.experimental.pallas import tpu as pltpu
from jax.sharding import PartitionSpec as P


GY = 16
GZ = 32
REACH = 4
SHIFTS = 4
LANES = 128

SIDE = 2 * REACH + 1
FACTORS = SIDE
HALF = LANES // 2


def plane_table():
    u = np.arange(HALF)
    h1 = (u + REACH) // SIDE
    h2 = u - SIDE * h1
    y, z = np.divmod(np.arange(GY * GZ), GZ)
    turns = (h1[None, :] * y[:, None] * GZ + h2[None, :] * z[:, None] * GY) % (GY * GZ)
    angle = 2.0 * np.pi * turns / (GY * GZ)
    used = (u <= (SIDE * SIDE) // 2)[None, :]
    whole = np.concatenate([np.cos(angle) * used, np.sin(angle) * used], axis=1).astype(np.float32)
    high = whole.astype(jnp.bfloat16)
    low = (whole - high.astype(np.float32)).astype(jnp.bfloat16)
    return np.concatenate([high, low], axis=1)


def turn_table(grid_x, count):
    middle = count * np.arange(2)[:, None] + (count - 1) / 2
    angle = 2.0 * np.pi * np.arange(1, REACH + 1)[None, :] * middle / grid_x
    return np.concatenate([np.cos(angle), np.sin(angle)], axis=1).astype(np.float32)


def column_index(waves):
    g0, flat = waves[:, 0], waves[:, 1] * SIDE + waves[:, 2]
    u = jnp.abs(flat)
    turn = jnp.where(flat < 0, -1, 1)
    side = jnp.sign(g0)
    cos_row = jnp.abs(g0) * LANES + u
    sin_row = jnp.where(g0 == 0, 0, REACH + jnp.abs(g0)) * LANES + u
    half = waves.shape[0] // 2

    def order(cosine, sine):
        return jnp.concatenate([cosine[:half], sine[:half], cosine[half:], sine[half:]])

    return jnp.stack(
        [
            order(cos_row, sin_row),
            order(sin_row + HALF, cos_row + HALF),
            order(jnp.ones_like(g0), side),
            order(-turn * side, turn),
        ]
    )


def vmem(count):
    return [pl.BlockSpec(memory_space=pltpu.VMEM)] * count


SMEM = pl.BlockSpec(memory_space=pltpu.SMEM)


def room(mebibytes):
    return pltpu.CompilerParams(vmem_limit_bytes=mebibytes << 20)


def prepare_kernel(stride, choices, table, energy, empty, occupied, choice, mine, theirs, sent, partner, level, sems):
    half = mine.shape[0]
    points = mine.shape[1]
    core = lax.axis_index("row") % 2
    parts = (core, 1 - core)
    copies = [
        pltpu.make_async_copy(empty.at[0, pl.ds(pl.multiple_of(part * half, half), half)], to, sems.at[i])
        for i, (part, to) in enumerate(zip(parts, (mine, theirs)))
    ]
    copies.append(pltpu.make_async_copy(occupied.at[0], sent.at[:, pl.ds(0, points)], sems.at[2]))
    small = [pltpu.make_async_copy(table, partner, sems.at[3]), pltpu.make_async_copy(energy, level, sems.at[4])]
    for copy in small + copies:
        copy.start()
    for copy in small:
        copy.wait()
    steps = [jnp.clip(partner[moment, 0] // stride, 1, choices) - 1 for moment in range(2)]
    choice[0, 0] = steps[0] * choices + steps[1]
    states = sent.shape[0]
    square = (states, states)
    here = lax.broadcasted_iota(jnp.int32, square, 0) == lax.broadcasted_iota(jnp.int32, square, 1)
    spread = jnp.where(here, jnp.broadcast_to(level[...].astype(jnp.float32), square), 0.0)
    column = jnp.sum(spread, axis=1, keepdims=True)
    sent[:, points:] = jnp.broadcast_to(column, (states, LANES)).astype(jnp.bfloat16)
    for copy in copies:
        copy.wait()


def prepare(partner, occ_energy, empty, occupied, stride, choices):
    _, bands, points = empty.shape
    states = occupied.shape[1]
    half = jax.ShapeDtypeStruct((bands // 2, points), jnp.bfloat16)
    return pl.pallas_call(
        functools.partial(prepare_kernel, stride, choices),
        out_shape=[
            jax.ShapeDtypeStruct((1, 1), jnp.int32),
            half,
            half,
            jax.ShapeDtypeStruct((states, points + LANES), jnp.bfloat16),
        ],
        in_specs=[pl.BlockSpec(memory_space=pltpu.HBM)] * 4,
        out_specs=[SMEM] + vmem(3),
        scratch_shapes=[
            pltpu.SMEM(partner.shape, partner.dtype),
            pltpu.VMEM(occ_energy.shape, occ_energy.dtype),
            pltpu.SemaphoreType.DMA((5,)),
        ],
        compiler_params=room(4),
        name="prepare",
    )(*[pltpu.with_memory_space_constraint(value, pltpu.HBM) for value in (partner, occ_energy, empty, occupied)])


def settle_kernel(count, *refs):
    for source, to in zip(refs[:count], refs[count:]):
        to[...] = source[...]


def settle(*blocks):
    return pl.pallas_call(
        functools.partial(settle_kernel, len(blocks)),
        out_shape=[jax.ShapeDtypeStruct(block.shape, block.dtype) for block in blocks],
        in_specs=vmem(len(blocks)),
        out_specs=vmem(len(blocks)),
        compiler_params=room(2),
        name="settle",
    )(*blocks)


def transform(emp, occ, plane, wide, density, part, after=None):
    bands, points = emp.shape
    states = occ.shape[0]
    sheet = plane.shape[0]
    count = points // sheet
    tile = 16
    if occ.dtype != jnp.float32:
        wide[...] = occ[:, :points].astype(jnp.float32)
        occ = wide

    def fill(v):
        for step in range(count):
            at = slice(step * sheet, (step + 1) * sheet)
            row = jnp.broadcast_to(occ[v : v + 1, at], (tile, sheet)).astype(jnp.bfloat16)
            for top in range(0, bands, tile):
                density[v % 2, step * bands + top : step * bands + top + tile, :] = row * emp[top : top + tile, at]

    fill(0)
    for v in range(states):
        if v + 1 < states:
            fill(v + 1)
        made = jnp.dot(density[v % 2], plane[...], preferred_element_type=jnp.float32)
        made = made[:, :LANES] + made[:, LANES:]
        for step in range(count):
            part[step, v * bands : (v + 1) * bands, :] = made[step * bands : (step + 1) * bands]
        if after is not None and v > 0:
            after(v - 1)
    if after is not None:
        after(states - 1)


def fold_pair(place, pair, turns, grid_x, near, far, bands, store):
    count = near.shape[0]
    lower = place[0] if pair == 0 else 1 - place[0]
    sign = (1 - 2 * place[1]).astype(jnp.float32)
    turn = {}
    for g in range(1, REACH + 1):
        scale = sign if g % 2 else 1.0
        turn[g] = turns[lower, g - 1] * scale, turns[lower, REACH + g - 1] * scale
    tall = 8

    def weighted(values, weights):
        total = values[0] * weights[0]
        for value, weight in zip(values[1:], weights[1:]):
            total = total + value * weight
        return total

    def after(v):
        for top in range(v * bands, (v + 1) * bands, tall):
            rows = slice(top, top + tall)
            ones = [near[step, rows, :] for step in range(count)]
            twos = [far[step, rows, :] for step in range(count)]
            for odd in (0, 1):
                both = [one - two if odd else one + two for one, two in zip(ones, twos)]
                half = count // 2
                evens = [both[half + i] + both[half - 1 - i] for i in range(half)]
                odds = [both[half + i] - both[half - 1 - i] for i in range(half)]
                if not odd:
                    store(0, rows, functools.reduce(lambda p, q: p + q, evens))
                for g in range(2 - odd, REACH + 1, 2):
                    angles = [2.0 * math.pi * g * (i + 0.5) / grid_x for i in range(half)]
                    even = weighted(evens, [math.cos(t) for t in angles])
                    rest = weighted(odds, [math.sin(t) for t in angles])
                    c, s = turn[g]
                    store(g, rows, even * c - rest * s)
                    store(REACH + g, rows, even * s + rest * c)

    return after


def first_kernel(emp, occ, plane, part, wide, density):
    transform(emp, occ, plane, wide, density, part)


def own_kernel(emp, occ, plane, index, part, matrix, wide, density):
    share = matrix.shape[0] // occ.shape[0]
    signs = index[2:4, :].astype(jnp.float32)

    def after(v):
        shape = (share, matrix.shape[1])
        rows = lax.broadcasted_iota(jnp.int32, shape, 0) + v * share
        two = jnp.where(rows == index[1:2, :], jnp.broadcast_to(signs[1:2], shape), 0.0)
        one = jnp.where(rows == index[0:1, :], jnp.broadcast_to(signs[0:1], shape), two)
        matrix[v * share : (v + 1) * share, :] = one.astype(jnp.bfloat16)

    transform(emp, occ, plane, wide, density, part, after)


def middle_pair_kernel(grid_x, place, turns, emp, occ, plane, near, total, wide, density, part):
    def store(j, rows, value):
        total[j, rows, :] = value

    transform(emp, occ, plane, wide, density, part, fold_pair(place, 0, turns, grid_x, near, part, emp.shape[0], store))


def last_pair_kernel(
    grid_x, scale, place, turns, emp, occ, plane, near, before, matrix, left, wide, density, part, total, narrow
):
    def store(j, rows, value):
        total[j, rows, :] = before[j, rows, :] + value

    transform(emp, occ, plane, wide, density, part, fold_pair(place, 1, turns, grid_x, near, part, emp.shape[0], store))
    for j in range(FACTORS):
        narrow[:, j * LANES : (j + 1) * LANES] = total[j].astype(jnp.bfloat16)
    proj = jnp.dot(narrow[...], matrix[...], preferred_element_type=jnp.float32)
    left[...] = (proj * scale).astype(jnp.bfloat16)


def scratch_of(emp, states):
    bands, points = emp.shape
    sheet = GY * GZ
    return [
        pltpu.VMEM((states, points), jnp.float32),
        pltpu.VMEM((2, points // sheet * bands, sheet), jnp.bfloat16),
    ]


def project_own(emp, occ, index):
    bands, points = emp.shape
    states = occ.shape[0]
    part_shape = (points // (GY * GZ), bands * states, LANES)
    return pl.pallas_call(
        own_kernel,
        out_shape=[
            jax.ShapeDtypeStruct(part_shape, jnp.float32),
            jax.ShapeDtypeStruct((FACTORS * LANES, index.shape[1]), jnp.bfloat16),
        ],
        in_specs=vmem(4),
        out_specs=vmem(2),
        scratch_shapes=scratch_of(emp, states),
        compiler_params=room(8),
        name="own",
    )(emp, occ, jnp.asarray(plane_table()), index)


def project(part_own, matrix, blocks, place, grid_x, scale):
    (core, x, far) = blocks
    bands, points = core[0].shape
    states = core[1].shape[0]
    pairs = bands * states
    count = points // (GY * GZ)
    columns = matrix.shape[1]
    plane = jnp.asarray(plane_table())
    turns = jnp.asarray(turn_table(grid_x, count))
    part_shape = (count, pairs, LANES)
    total_shape = (FACTORS, pairs, LANES)
    scratch = scratch_of(core[0], states)
    part = pltpu.VMEM(part_shape, jnp.float32)
    part_core = pl.pallas_call(
        first_kernel,
        out_shape=jax.ShapeDtypeStruct(part_shape, jnp.float32),
        in_specs=vmem(3),
        out_specs=vmem(1)[0],
        scratch_shapes=scratch,
        compiler_params=room(6),
        name="core",
    )(*core, plane)
    total = pl.pallas_call(
        functools.partial(middle_pair_kernel, grid_x),
        out_shape=jax.ShapeDtypeStruct(total_shape, jnp.float32),
        in_specs=[SMEM, SMEM] + vmem(4),
        out_specs=vmem(1)[0],
        scratch_shapes=scratch + [part],
        compiler_params=room(8),
        name="pair",
    )(place, turns, *x, plane, part_own)
    return pl.pallas_call(
        functools.partial(last_pair_kernel, grid_x, scale),
        out_shape=jax.ShapeDtypeStruct((pairs, columns), jnp.bfloat16),
        in_specs=[SMEM, SMEM] + vmem(6),
        out_specs=vmem(1)[0],
        scratch_shapes=scratch
        + [part, pltpu.VMEM(total_shape, jnp.float32), pltpu.VMEM((pairs, FACTORS * LANES), jnp.bfloat16)],
        compiler_params=room(14),
        name="last",
    )(place, turns, *far, plane, part_core, total, matrix)


def gram_of(core, values, weights):
    width = values.shape[1] // 2
    at = pl.multiple_of(core * width, LANES)
    right = [
        (values[:, pl.ds(at + tile * LANES, LANES)].astype(jnp.float32) * weights[...]).astype(jnp.bfloat16)
        for tile in range(width // LANES)
    ]
    return lax.dot_general(
        values[...], jnp.concatenate(right, axis=1), (((0,), (0,)), ((), ())), preferred_element_type=jnp.float32
    )


def gram_own_kernel(place, own, w_own, gram):
    gram[...] = gram_of(place[0], own, w_own)


def roll_half(value):
    return pltpu.roll(value, value.shape[1] // 2, 1)


def gram_kernel(place, first, other, w_other, keep, to_y, to_x, to_xy, gram):
    core, x, y = place[0], place[1], place[2]
    gram[...] = first[...] + gram_of(core, other, w_other)
    rows = gram.shape[0] // 8
    order = (0, 2, 1, 3)
    low = lax.broadcasted_iota(jnp.int32, (rows, gram.shape[1]), 1) < gram.shape[1] // 2

    def quadrant(way, zl):
        lower = gram[pl.ds(pl.multiple_of(order[zl] * 2 * rows + way * rows, 8), rows), :]
        upper = gram[pl.ds(pl.multiple_of(order[2 + zl] * 2 * rows + way * rows, 8), rows), :]
        return jnp.where(low, lower, roll_half(upper)), jnp.where(low, roll_half(lower), upper)

    for zl in range(2):
        at = slice(zl * rows, (zl + 1) * rows)
        for way, near, far in ((y, keep, to_x), (1 - y, to_y, to_xy)):
            zero, one = quadrant(way, zl)
            near[at, :] = jnp.where(x == 0, zero, one).astype(near.dtype)
            far[at, :] = jnp.where(x == 0, one, zero).astype(far.dtype)


def middle_kernel(place, keep, from_y, from_x, from_xy, stay, *refs):
    sends, block = refs[:3], refs[3]
    x, z = place[1], place[3]
    rows = keep.shape[0] // 2
    low = lax.broadcasted_iota(jnp.int32, (rows, keep.shape[1]), 1) < keep.shape[1] // 2
    for zl in range(2):
        at = slice(zl * rows, (zl + 1) * rows)
        same = keep[at, :] + from_y[at, :].astype(jnp.float32)
        cross = from_x[at, :].astype(jnp.float32) + from_xy[at, :].astype(jnp.float32)
        zero = jnp.where(x == 0, same, cross)
        one = jnp.where(x == 0, cross, same)
        block[zl] = jnp.where(low, zero, roll_half(one))
        block[2 + zl] = jnp.where(low, roll_half(zero), one)
    stay[...] = block[z]
    for index, send in enumerate(sends):
        send[...] = block[z ^ (index + 1)].astype(send.dtype)


def final_kernel(stay, one, two, three, out):
    total = stay[...] + one[...].astype(jnp.float32)
    total = total + two[...].astype(jnp.float32) + three[...].astype(jnp.float32)
    width = total.shape[1] // 2
    out[0] = total[:, :width]
    out[1] = roll_half(total)[:, :width]


def reduce_near(place, own, other, w_own, w_other):
    wide = own.shape[1]
    kcount, rcount = lax.axis_size("ka"), lax.axis_size("row")
    quarter = (wide // 4, wide // 2)
    first = pl.pallas_call(
        gram_own_kernel,
        out_shape=jax.ShapeDtypeStruct((wide, wide // 2), jnp.float32),
        in_specs=[SMEM] + vmem(2),
        out_specs=vmem(1)[0],
        compiler_params=room(8),
        name="gram_own",
    )(place, own, w_own)
    keep, to_y, to_x, to_xy = pl.pallas_call(
        gram_kernel,
        out_shape=[jax.ShapeDtypeStruct(quarter, d) for d in (jnp.float32, jnp.bfloat16, jnp.bfloat16, jnp.bfloat16)],
        in_specs=[SMEM] + vmem(3),
        out_specs=vmem(4),
        scratch_shapes=[pltpu.VMEM((wide, wide // 2), jnp.float32)],
        compiler_params=room(10),
        name="gram",
    )(place, first, other, w_other)

    def route(dy, dx):
        return [(k * rcount + r, (k ^ dy) * rcount + (r ^ dx)) for k in range(kcount) for r in range(rcount)]

    both = ("ka", "row")
    from_y = lax.ppermute(to_y, both, route(1, 0))
    from_xy = lax.ppermute(to_xy, both, route(1, 2))
    from_x = lax.ppermute(to_x, both, route(0, 2))
    piece = (quarter[0] // 2, quarter[1])
    stay, *sends = pl.pallas_call(
        middle_kernel,
        out_shape=[jax.ShapeDtypeStruct(piece, jnp.float32)] + [jax.ShapeDtypeStruct(piece, jnp.bfloat16)] * 3,
        in_specs=[SMEM] + vmem(4),
        out_specs=vmem(4),
        scratch_shapes=[pltpu.VMEM((4,) + piece, jnp.float32)],
        compiler_params=room(6),
        name="middle",
    )(place, keep, from_y, from_x, from_xy)
    arrived = [lax.ppermute(send, both, route(2 * (m + 1), 0)) for m, send in enumerate(sends)]
    return pl.pallas_call(
        final_kernel,
        out_shape=jax.ShapeDtypeStruct((2, piece[0], piece[1] // 2), jnp.float32),
        in_specs=vmem(4),
        out_specs=vmem(1)[0],
        compiler_params=room(4),
        name="final",
    )(stay, *arrived)


def reduce_far(place, own, other, w_own, w_other):
    kcount = lax.axis_size("ka")
    wide = own.shape[1]
    width = wide // 4
    left = jnp.concatenate([own, other], axis=0)
    weight = jnp.concatenate([w_own[:, :1], w_other[:, :1]], axis=0)
    right = lax.dynamic_slice_in_dim(left, place[0] * 2 * width, 2 * width, 1)
    right = (right.astype(jnp.float32) * weight).astype(jnp.bfloat16)
    gram = lax.dot_general(left, right, (((0,), (0,)), ((), ())), preferred_element_type=jnp.float32)
    gram = gram.reshape(2, 2, width, 2, width).swapaxes(0, 1).reshape(kcount, wide // kcount, 2, width)
    parts = lax.all_to_all(gram.astype(jnp.bfloat16), "ka", 0, 0, tiled=True)
    total = jnp.sum(parts.astype(jnp.float32), axis=0)
    mine = lax.dynamic_index_in_dim(total, place[1], 1, keepdims=False)
    send = lax.dynamic_index_in_dim(total, 1 - place[1], 1, keepdims=False)
    came = lax.ppermute(send, "row", [(r, r ^ 2) for r in range(lax.axis_size("row"))])
    first = place[1] == 0
    return jnp.stack([jnp.where(first, mine, came), jnp.where(first, came, mine)])


def per_device(occupied, empty, occ_energy, emp_energy, partner, gvecs):
    kcount, rcount = lax.axis_size("ka"), lax.axis_size("row")
    assert rcount == 4 and partner.shape[0] == 2
    k, r = lax.axis_index("ka"), lax.axis_index("row")
    x, core = r // 2, r % 2
    points = occupied.shape[2]
    grid_x = points * rcount // (GY * GZ)
    stride = kcount // min(SHIFTS, kcount)
    choices = min(SHIFTS, kcount) - 1
    half = empty.shape[1] // 2
    choice, mine, theirs, sent = prepare(partner, occ_energy, empty, occupied, stride, choices)
    emp_x = lax.ppermute(mine, "row", [(i, i ^ 2) for i in range(rcount)])
    emp_xc = lax.ppermute(theirs, "row", [(i, i ^ 3) for i in range(rcount)])
    emp_c = lax.ppermute(theirs, "row", [(i, i ^ 1) for i in range(rcount)])

    states = occupied.shape[1]

    swap = [(i, i ^ 1) for i in range(rcount)]

    def fetch(shift, operands):
        block, waves = operands

        def route(dx):
            pairs = []
            for i in range(kcount):
                for j in range(rcount):
                    to = j ^ dx
                    pairs.append((i * rcount + j, (i + shift[to // 2] * stride) % kcount * rcount + to))
            return pairs

        both = ("ka", "row")
        near = lax.ppermute(block, both, route(0))
        far = lax.ppermute(block, both, route(2))
        near_c = lax.ppermute(near, "row", swap)
        index = column_index(lax.dynamic_index_in_dim(waves, x, 0, keepdims=False))
        return settle(near, near_c, far, index)

    branches = [functools.partial(fetch, (one + 1, two + 1)) for one in range(choices) for two in range(choices)]
    occ_own, occ_c, occ_x, index = lax.switch(choice[0, 0], branches, (sent, gvecs))
    occ_xc = lax.ppermute(occ_x, "row", swap)

    place = jnp.stack([core, x, k % 2, k // 2]).astype(jnp.int32)
    part_own, matrix = project_own(mine, occ_own, index)
    blocks = ((emp_c, occ_c), (emp_x, occ_x), (emp_xc, occ_xc))
    left = project(part_own, matrix, blocks, place, grid_x, 1.0 / (points * rcount))
    level = occ_own[:, points : points + 1].astype(jnp.float32)

    def weights(which):
        energy = lax.dynamic_slice_in_dim(emp_energy[0], which * half, half, 0).astype(jnp.float32)
        value = 1.0 / (energy[None, :] - level)
        return jnp.broadcast_to(value.reshape(states * half, 1), (states * half, LANES))

    w_own, w_other = weights(core), weights(1 - core)
    other = lax.ppermute(left, "row", swap)
    reduce = reduce_near if kcount == 8 else reduce_far
    return reduce(place, left, other, w_own, w_other)


def solution(mesh):
    placed = (P("ka", None, "row"), P("ka", None, "row"), P("ka", None), P("ka", None), P(), P())

    return jax.shard_map(per_device, mesh=mesh, in_specs=placed, out_specs=P(None, "ka", "row"), check_vma=False)
```

```python
import functools
import math

import jax
import jax.numpy as jnp
import numpy as np
from jax import lax
from jax.experimental import pallas as pl
from jax.experimental.pallas import tpu as pltpu
from jax.sharding import PartitionSpec as P


GY = 16
GZ = 32
REACH = 4
SHIFTS = 4
LANES = 128

SIDE = 2 * REACH + 1
FACTORS = SIDE
HALF = LANES // 2


def plane_table():
    u = np.arange(HALF)
    h1 = (u + REACH) // SIDE
    h2 = u - SIDE * h1
    y, z = np.divmod(np.arange(GY * GZ), GZ)
    turns = (h1[None, :] * y[:, None] * GZ + h2[None, :] * z[:, None] * GY) % (GY * GZ)
    angle = 2.0 * np.pi * turns / (GY * GZ)
    used = (u <= (SIDE * SIDE) // 2)[None, :]
    whole = np.concatenate([np.cos(angle) * used, np.sin(angle) * used], axis=1).astype(np.float32)
    high = whole.astype(jnp.bfloat16)
    low = (whole - high.astype(np.float32)).astype(jnp.bfloat16)
    return np.concatenate([high, low], axis=1)


def column_index(waves):
    g0, flat = waves[:, 0], waves[:, 1] * SIDE + waves[:, 2]
    u = jnp.abs(flat)
    turn = jnp.where(flat < 0, -1, 1)
    side = jnp.sign(g0)
    cos_row = jnp.abs(g0) * LANES + u
    sin_row = jnp.where(g0 == 0, 0, REACH + jnp.abs(g0)) * LANES + u
    half = waves.shape[0] // 2

    def order(cosine, sine):
        return jnp.concatenate([cosine[:half], sine[:half], cosine[half:], sine[half:]])

    return jnp.stack(
        [
            order(cos_row, sin_row),
            order(sin_row + HALF, cos_row + HALF),
            order(jnp.ones_like(g0), side),
            order(-turn * side, turn),
        ]
    )


def vmem(count):
    return [pl.BlockSpec(memory_space=pltpu.VMEM)] * count


SMEM = pl.BlockSpec(memory_space=pltpu.SMEM)


def room(mebibytes):
    return pltpu.CompilerParams(vmem_limit_bytes=mebibytes << 20)


def prepare_kernel(stride, choices, table, energy, empty, occupied, choice, mine, theirs, sent, partner, level, sems):
    half = mine.shape[0]
    points = mine.shape[1]
    core = lax.axis_index("row") % 2
    parts = (core, 1 - core)
    copies = [
        pltpu.make_async_copy(empty.at[0, pl.ds(pl.multiple_of(part * half, half), half)], to, sems.at[i])
        for i, (part, to) in enumerate(zip(parts, (mine, theirs)))
    ]
    copies.append(pltpu.make_async_copy(occupied.at[0], sent.at[:, pl.ds(0, points)], sems.at[2]))
    small = [pltpu.make_async_copy(table, partner, sems.at[3]), pltpu.make_async_copy(energy, level, sems.at[4])]
    for copy in small + copies:
        copy.start()
    for copy in small:
        copy.wait()
    steps = [jnp.clip(partner[moment, 0] // stride, 1, choices) - 1 for moment in range(2)]
    choice[0, 0] = steps[0] * choices + steps[1]
    states = sent.shape[0]
    square = (states, states)
    here = lax.broadcasted_iota(jnp.int32, square, 0) == lax.broadcasted_iota(jnp.int32, square, 1)
    spread = jnp.where(here, jnp.broadcast_to(level[...].astype(jnp.float32), square), 0.0)
    column = jnp.sum(spread, axis=1, keepdims=True)
    sent[:, points:] = jnp.broadcast_to(column, (states, LANES)).astype(jnp.bfloat16)
    for copy in copies:
        copy.wait()


def prepare(partner, occ_energy, empty, occupied, stride, choices):
    _, bands, points = empty.shape
    states = occupied.shape[1]
    half = jax.ShapeDtypeStruct((bands // 2, points), jnp.bfloat16)
    return pl.pallas_call(
        functools.partial(prepare_kernel, stride, choices),
        out_shape=[
            jax.ShapeDtypeStruct((1, 1), jnp.int32),
            half,
            half,
            jax.ShapeDtypeStruct((states, points + LANES), jnp.bfloat16),
        ],
        in_specs=[pl.BlockSpec(memory_space=pltpu.HBM)] * 4,
        out_specs=[SMEM] + vmem(3),
        scratch_shapes=[
            pltpu.SMEM(partner.shape, partner.dtype),
            pltpu.VMEM(occ_energy.shape, occ_energy.dtype),
            pltpu.SemaphoreType.DMA((5,)),
        ],
        compiler_params=room(4),
        name="prepare",
    )(*[pltpu.with_memory_space_constraint(value, pltpu.HBM) for value in (partner, occ_energy, empty, occupied)])


def settle_kernel(count, *refs):
    for source, to in zip(refs[:count], refs[count:]):
        to[...] = source[...]


def settle(*blocks):
    return pl.pallas_call(
        functools.partial(settle_kernel, len(blocks)),
        out_shape=[pltpu.VMEM(block.shape, block.dtype) for block in blocks],
        in_specs=vmem(len(blocks)),
        out_specs=vmem(len(blocks)),
        compiler_params=room(2),
        name="settle",
    )(*blocks)


def whereabouts():
    r, k = lax.axis_index("row"), lax.axis_index("ka")
    return r % 2, r // 2, k % 2, k // 2


def transform(emp, occ, plane, wide, density, part, after=None):
    bands, points = emp.shape
    states = occ.shape[0]
    sheet = plane.shape[0]
    count = points // sheet
    tile = 16
    if occ.dtype != jnp.float32:
        wide[...] = occ[:, :points].astype(jnp.float32)
        occ = wide

    def fill(v):
        for step in range(count):
            at = slice(step * sheet, (step + 1) * sheet)
            row = jnp.broadcast_to(occ[v : v + 1, at], (tile, sheet)).astype(jnp.bfloat16)
            for top in range(0, bands, tile):
                density[v % 2, step * bands + top : step * bands + top + tile, :] = row * emp[top : top + tile, at]

    fill(0)
    for v in range(states):
        if v + 1 < states:
            fill(v + 1)
        made = jnp.dot(density[v % 2], plane[...], preferred_element_type=jnp.float32)
        made = made[:, :LANES] + made[:, LANES:]
        for step in range(count):
            part[step, v * bands : (v + 1) * bands, :] = made[step * bands : (step + 1) * bands]
        if after is not None and v > 0:
            after(v - 1)
    if after is not None:
        after(states - 1)


def fold_pair(pair, grid_x, near, far, bands, store):
    count = near.shape[0]
    core, x, _, _ = whereabouts()
    lower = core if pair == 0 else 1 - core
    sign = jnp.where(x == 0, jnp.float32(1), jnp.float32(-1))
    middle = (count - 1) / 2
    turn = {}
    for g in range(1, REACH + 1):
        angles = [2.0 * math.pi * g * (row * count + middle) / grid_x for row in range(2)]
        scale = sign if g % 2 else jnp.float32(1)
        turn[g] = [
            jnp.where(lower == 0, jnp.float32(part(angles[0])), jnp.float32(part(angles[1]))) * scale
            for part in (math.cos, math.sin)
        ]
    tall = 8

    def weighted(values, weights):
        total = values[0] * weights[0]
        for value, weight in zip(values[1:], weights[1:]):
            total = total + value * weight
        return total

    def after(v):
        for top in range(v * bands, (v + 1) * bands, tall):
            rows = slice(top, top + tall)
            ones = [near[step, rows, :] for step in range(count)]
            twos = [far[step, rows, :] for step in range(count)]
            for odd in (0, 1):
                both = [one - two if odd else one + two for one, two in zip(ones, twos)]
                half = count // 2
                evens = [both[half + i] + both[half - 1 - i] for i in range(half)]
                odds = [both[half + i] - both[half - 1 - i] for i in range(half)]
                if not odd:
                    store(0, rows, functools.reduce(lambda p, q: p + q, evens))
                for g in range(2 - odd, REACH + 1, 2):
                    angles = [2.0 * math.pi * g * (i + 0.5) / grid_x for i in range(half)]
                    even = weighted(evens, [math.cos(t) for t in angles])
                    rest = weighted(odds, [math.sin(t) for t in angles])
                    c, s = turn[g]
                    store(g, rows, even * c - rest * s)
                    store(REACH + g, rows, even * s + rest * c)

    return after


def first_kernel(emp, occ, plane, part, wide, density):
    transform(emp, occ, plane, wide, density, part)


def own_kernel(emp, occ, plane, energy, part, w_own, w_other, wide, density):
    bands, points = emp.shape
    states = occ.shape[0]
    core = whereabouts()[0]
    shape = (bands, energy.shape[1])
    down = lax.broadcasted_iota(jnp.int32, shape, 0)
    along = lax.broadcasted_iota(jnp.int32, shape, 1)
    levels = jnp.broadcast_to(energy[...].astype(jnp.float32), shape)
    for part_of, weight in ((core, w_own), (1 - core, w_other)):
        column = jnp.sum(jnp.where(along == down + part_of * bands, levels, 0.0), axis=1, keepdims=True)
        column = jnp.broadcast_to(column, (bands, LANES))
        for v in range(states):
            level = occ[v : v + 1, points : points + LANES].astype(jnp.float32)
            weight[v * bands : (v + 1) * bands, :] = 1.0 / (column - level)
    transform(emp, occ, plane, wide, density, part)


def matrix_kernel(index, matrix):
    share = 2 * LANES // 4
    shape = (share, matrix.shape[1])
    signs = index[2:4, :].astype(jnp.float32)

    def body(at, carry):
        start = pl.multiple_of(at * share, share)
        rows = lax.broadcasted_iota(jnp.int32, shape, 0) + start
        two = jnp.where(rows == index[1:2, :], jnp.broadcast_to(signs[1:2], shape), 0.0)
        one = jnp.where(rows == index[0:1, :], jnp.broadcast_to(signs[0:1], shape), two)
        matrix[pl.ds(start, share), :] = one.astype(jnp.bfloat16)
        return carry

    lax.fori_loop(0, matrix.shape[0] // share, body, 0)


def make_matrix(index):
    return pl.pallas_call(
        matrix_kernel,
        out_shape=pltpu.VMEM((FACTORS * LANES, index.shape[1]), jnp.bfloat16),
        in_specs=vmem(1),
        out_specs=vmem(1)[0],
        compiler_params=room(4),
        name="matrix",
    )(index)


def fold_pair(pair, grid_x, near, far, bands, store):
    count = near.shape[0]
    core, x, _, _ = whereabouts()
    lower = core if pair == 0 else 1 - core
    sign = jnp.where(x == 0, jnp.float32(1), jnp.float32(-1))
    middle = (count - 1) / 2
    turn = {}
    for g in range(1, REACH + 1):
        angles = [2.0 * math.pi * g * (row * count + middle) / grid_x for row in range(2)]
        scale = sign if g % 2 else jnp.float32(1)
        turn[g] = [
            jnp.where(lower == 0, jnp.float32(part(angles[0])), jnp.float32(part(angles[1]))) * scale
            for part in (math.cos, math.sin)
        ]
    tall = 8

    def weighted(values, weights):
        total = values[0] * weights[0]
        for value, weight in zip(values[1:], weights[1:]):
            total = total + value * weight
        return total

    def after(v):
        for top in range(v * bands, (v + 1) * bands, tall):
            rows = slice(top, top + tall)
            ones = [near[step, rows, :] for step in range(count)]
            twos = [far[step, rows, :] for step in range(count)]
            for odd in (0, 1):
                both = [one - two if odd else one + two for one, two in zip(ones, twos)]
                half = count // 2
                evens = [both[half + i] + both[half - 1 - i] for i in range(half)]
                odds = [both[half + i] - both[half - 1 - i] for i in range(half)]
                if not odd:
                    store(0, rows, functools.reduce(lambda p, q: p + q, evens))
                for g in range(2 - odd, REACH + 1, 2):
                    angles = [2.0 * math.pi * g * (i + 0.5) / grid_x for i in range(half)]
                    even = weighted(evens, [math.cos(t) for t in angles])
                    rest = weighted(odds, [math.sin(t) for t in angles])
                    c, s = turn[g]
                    store(g, rows, even * c - rest * s)
                    store(REACH + g, rows, even * s + rest * c)

    return after


def first_kernel(emp, occ, plane, part, wide, density):
    transform(emp, occ, plane, wide, density, part)


def middle_pair_kernel(grid_x, emp, occ, plane, near, total, wide, density, part):
    def store(j, rows, value):
        total[j, rows, :] = value

    transform(emp, occ, plane, wide, density, part, fold_pair(0, grid_x, near, part, emp.shape[0], store))


def last_pair_kernel(
    grid_x, scale, emp, occ, plane, near, before, matrix, left, wide, density, part, total, narrow
):
    def store(j, rows, value):
        total[j, rows, :] = before[j, rows, :] + value

    transform(emp, occ, plane, wide, density, part, fold_pair(1, grid_x, near, part, emp.shape[0], store))
    for j in range(FACTORS):
        narrow[:, j * LANES : (j + 1) * LANES] = total[j].astype(jnp.bfloat16)
    proj = jnp.dot(narrow[...], matrix[...], preferred_element_type=jnp.float32)
    left[...] = (proj * scale).astype(jnp.bfloat16)


def scratch_of(emp, states):
    bands, points = emp.shape
    sheet = GY * GZ
    return [
        pltpu.VMEM((states, points), jnp.float32),
        pltpu.VMEM((2, points // sheet * bands, sheet), jnp.bfloat16),
    ]


def project(matrix, blocks, energy, grid_x, scale):
    (own, core, x, far) = blocks
    bands, points = core[0].shape
    states = core[1].shape[0]
    pairs = bands * states
    count = points // (GY * GZ)
    columns = matrix.shape[1]
    plane = jnp.asarray(plane_table())
    part_shape = (count, pairs, LANES)
    total_shape = (FACTORS, pairs, LANES)
    scratch = scratch_of(core[0], states)
    part = pltpu.VMEM(part_shape, jnp.float32)

    def first(kernel, outs, operands):
        return pl.pallas_call(
            kernel,
            out_shape=[jax.ShapeDtypeStruct(shape, jnp.float32) for shape in outs],
            in_specs=vmem(len(operands)),
            out_specs=vmem(len(outs)),
            scratch_shapes=scratch,
            compiler_params=room(6),
        )(*operands)

    weight_shape = (pairs, LANES)
    part_own, w_own, w_other = first(own_kernel, [part_shape] + [weight_shape] * 2, (*own, plane, energy))
    (part_core,) = first(first_kernel, [part_shape], (*core, plane))
    total = pl.pallas_call(
        functools.partial(middle_pair_kernel, grid_x),
        out_shape=jax.ShapeDtypeStruct(total_shape, jnp.float32),
        in_specs=vmem(4),
        out_specs=vmem(1)[0],
        scratch_shapes=scratch + [part],
        compiler_params=room(8),
        name="pair",
    )(*x, plane, part_own)
    left = pl.pallas_call(
        functools.partial(last_pair_kernel, grid_x, scale),
        out_shape=jax.ShapeDtypeStruct((pairs, columns), jnp.bfloat16),
        in_specs=vmem(6),
        out_specs=vmem(1)[0],
        scratch_shapes=scratch
        + [part, pltpu.VMEM(total_shape, jnp.float32), pltpu.VMEM((pairs, FACTORS * LANES), jnp.bfloat16)],
        compiler_params=room(14),
        name="last",
    )(*far, plane, part_core, total, matrix)
    return left, w_own, w_other


def gram_of(core, values, weights):
    width = values.shape[1] // 2
    at = pl.multiple_of(core * width, LANES)
    right = [
        (values[:, pl.ds(at + tile * LANES, LANES)].astype(jnp.float32) * weights[...]).astype(jnp.bfloat16)
        for tile in range(width // LANES)
    ]
    return lax.dot_general(
        values[...], jnp.concatenate(right, axis=1), (((0,), (0,)), ((), ())), preferred_element_type=jnp.float32
    )


def gram_own_kernel(own, w_own, gram):
    gram[...] = gram_of(whereabouts()[0], own, w_own)


def roll_half(value):
    return pltpu.roll(value, value.shape[1] // 2, 1)


def gram_kernel(first, other, w_other, keep, to_y, to_z, to_yz, gram):
    core, _, y, z = whereabouts()
    zl = z % 2
    gram[...] = first[...] + gram_of(core, other, w_other)
    rows = gram.shape[0] // 8
    for out, to_y_of, to_zl in ((keep, y, zl), (to_y, 1 - y, zl), (to_z, y, 1 - zl), (to_yz, 1 - y, 1 - zl)):
        for zh in range(2):
            start = ((2 * to_zl + zh) * 2 + to_y_of) * rows
            out[zh * rows : (zh + 1) * rows, :] = gram[pl.ds(pl.multiple_of(start, 8), rows), :].astype(out.dtype)


def middle_kernel(keep, from_y, from_z, from_yz, stay, to_x, to_z, to_xz, total):
    _, x, _, z = whereabouts()
    zh = z // 2
    rows = keep.shape[0] // 2
    total[...] = (keep[...] + from_y[...].astype(jnp.float32)) + (
        from_z[...].astype(jnp.float32) + from_yz[...].astype(jnp.float32)
    )
    low = lax.broadcasted_iota(jnp.int32, (rows // 2, keep.shape[1]), 1) < keep.shape[1] // 2
    for to_zh, near, far in ((zh, stay, to_x), (1 - zh, to_z, to_xz)):
        top = total[pl.ds(pl.multiple_of(to_zh * rows, 8), rows // 2), :]
        bottom = total[pl.ds(pl.multiple_of(to_zh * rows + rows // 2, 8), rows // 2), :]
        zero = jnp.where(low, top, roll_half(bottom))
        one = jnp.where(low, roll_half(top), bottom)
        near[...] = jnp.where(x == 0, zero, one).astype(near.dtype)
        far[...] = jnp.where(x == 0, one, zero).astype(far.dtype)


def final_kernel(stay, from_x, from_z, from_xz, out):
    x = whereabouts()[1]
    same = stay[...] + from_z[...].astype(jnp.float32)
    cross = from_x[...].astype(jnp.float32) + from_xz[...].astype(jnp.float32)
    rows, width = same.shape[0], same.shape[1] // 2
    for moment in range(2):
        value = jnp.where(x == moment, same, cross)
        out[moment, :rows, :] = value[:, :width]
        out[moment, rows:, :] = roll_half(value)[:, :width]


def reduce_near(own, other, w_own, w_other):
    wide = own.shape[1]
    kcount, rcount = lax.axis_size("ka"), lax.axis_size("row")
    bf16, f32 = jnp.bfloat16, jnp.float32
    first = pl.pallas_call(
        gram_own_kernel,
        out_shape=jax.ShapeDtypeStruct((wide, wide // 2), f32),
        in_specs=vmem(2),
        out_specs=vmem(1)[0],
        compiler_params=room(8),
        name="gram_own",
    )(own, w_own)
    quarter = (wide // 4, wide // 2)
    keep, *sends = pl.pallas_call(
        gram_kernel,
        out_shape=[jax.ShapeDtypeStruct(quarter, d) for d in (f32, bf16, bf16, bf16)],
        in_specs=vmem(3),
        out_specs=vmem(4),
        scratch_shapes=[pltpu.VMEM((wide, wide // 2), f32)],
        compiler_params=room(10),
        name="gram",
    )(first, other, w_other)

    def exchange(values, ways):
        came = []
        for value, (dk, dr) in zip(values, ways):
            pairs = [(k * rcount + r, (k ^ dk) * rcount + (r ^ dr)) for k in range(kcount) for r in range(rcount)]
            came.append(lax.ppermute(value, ("ka", "row"), pairs))
        return came

    came = exchange(sends, ((1, 0), (2, 0), (3, 0)))
    piece = (quarter[0] // 4, quarter[1])
    stay, *sends = pl.pallas_call(
        middle_kernel,
        out_shape=[jax.ShapeDtypeStruct(piece, d) for d in (f32, bf16, bf16, bf16)],
        in_specs=vmem(4),
        out_specs=vmem(4),
        scratch_shapes=[pltpu.VMEM(quarter, f32)],
        compiler_params=room(6),
        name="middle",
    )(keep, *came)
    came = exchange(sends, ((0, 2), (4, 0), (4, 2)))
    return pl.pallas_call(
        final_kernel,
        out_shape=jax.ShapeDtypeStruct((2, piece[0] * 2, piece[1] // 2), f32),
        in_specs=vmem(4),
        out_specs=vmem(1)[0],
        compiler_params=room(4),
        name="final",
    )(stay, *came)


def reduce_far(own, other, w_own, w_other):
    kcount = lax.axis_size("ka")
    core, x, _, _ = whereabouts()
    wide = own.shape[1]
    width = wide // 4
    left = jnp.concatenate([own, other], axis=0)
    weight = jnp.concatenate([w_own[:, :1], w_other[:, :1]], axis=0)
    right = lax.dynamic_slice_in_dim(left, core * 2 * width, 2 * width, 1)
    right = (right.astype(jnp.float32) * weight).astype(jnp.bfloat16)
    gram = lax.dot_general(left, right, (((0,), (0,)), ((), ())), preferred_element_type=jnp.float32)
    gram = gram.reshape(2, 2, width, 2, width).swapaxes(0, 1).reshape(kcount, wide // kcount, 2, width)
    parts = lax.all_to_all(gram.astype(jnp.bfloat16), "ka", 0, 0, tiled=True)
    total = jnp.sum(parts.astype(jnp.float32), axis=0)
    mine = lax.dynamic_index_in_dim(total, x, 1, keepdims=False)
    send = lax.dynamic_index_in_dim(total, 1 - x, 1, keepdims=False)
    came = lax.ppermute(send, "row", [(r, r ^ 2) for r in range(lax.axis_size("row"))])
    first = x == 0
    return jnp.stack([jnp.where(first, mine, came), jnp.where(first, came, mine)])


def per_device(occupied, empty, occ_energy, emp_energy, partner, gvecs):
    kcount, rcount = lax.axis_size("ka"), lax.axis_size("row")
    assert rcount == 4 and partner.shape[0] == 2
    r = lax.axis_index("row")
    x = r // 2
    points = occupied.shape[2]
    grid_x = points * rcount // (GY * GZ)
    stride = kcount // min(SHIFTS, kcount)
    choices = min(SHIFTS, kcount) - 1
    choice, mine, theirs, sent = prepare(partner, occ_energy, empty, occupied, stride, choices)
    emp_x = lax.ppermute(mine, "row", [(i, i ^ 2) for i in range(rcount)])
    emp_xc = lax.ppermute(theirs, "row", [(i, i ^ 3) for i in range(rcount)])
    emp_c = lax.ppermute(theirs, "row", [(i, i ^ 1) for i in range(rcount)])

    swap = [(i, i ^ 1) for i in range(rcount)]

    def fetch(shift, operands):
        block, waves = operands

        def route(dx):
            pairs = []
            for i in range(kcount):
                for j in range(rcount):
                    to = j ^ dx
                    pairs.append((i * rcount + j, (i + shift[to // 2] * stride) % kcount * rcount + to))
            return pairs

        both = ("ka", "row")
        far = lax.ppermute(block, both, route(2))
        near = lax.ppermute(block, both, route(0))
        near_c = lax.ppermute(near, "row", swap)
        matrix = make_matrix(column_index(lax.dynamic_index_in_dim(waves, x, 0, keepdims=False)))
        return *settle(near, near_c, far), matrix

    branches = [functools.partial(fetch, (one + 1, two + 1)) for one in range(choices) for two in range(choices)]
    occ_own, occ_c, occ_x, matrix = lax.switch(choice[0, 0], branches, (sent, gvecs))
    occ_xc = lax.ppermute(occ_x, "row", swap)

    blocks = ((mine, occ_own), (emp_c, occ_c), (emp_x, occ_x), (emp_xc, occ_xc))
    left, w_own, w_other = project(matrix, blocks, emp_energy, grid_x, 1.0 / (points * rcount))
    other = lax.ppermute(left, "row", swap)
    reduce = reduce_near if kcount == 8 else reduce_far
    return reduce(left, other, w_own, w_other)


def solution(mesh):
    placed = (P("ka", None, "row"), P("ka", None, "row"), P("ka", None), P("ka", None), P(), P())

    return jax.shard_map(per_device, mesh=mesh, in_specs=placed, out_specs=P(None, "ka", "row"), check_vma=False)
```

```python
import functools
import math

import jax
import jax.numpy as jnp
import numpy as np
from jax import lax
from jax.experimental import pallas as pl
from jax.experimental.pallas import tpu as pltpu
from jax.sharding import PartitionSpec as P


GY = 16
GZ = 32
REACH = 4
SHIFTS = 4
LANES = 128

SIDE = 2 * REACH + 1
FACTORS = SIDE
HALF = LANES // 2


def plane_table():
    u = np.arange(HALF)
    h1 = (u + REACH) // SIDE
    h2 = u - SIDE * h1
    y, z = np.divmod(np.arange(GY * GZ), GZ)
    turns = (h1[None, :] * y[:, None] * GZ + h2[None, :] * z[:, None] * GY) % (GY * GZ)
    angle = 2.0 * np.pi * turns / (GY * GZ)
    used = (u <= (SIDE * SIDE) // 2)[None, :]
    whole = np.concatenate([np.cos(angle) * used, np.sin(angle) * used], axis=1).astype(np.float32)
    high = whole.astype(jnp.bfloat16)
    low = (whole - high.astype(np.float32)).astype(jnp.bfloat16)
    return np.concatenate([high, low], axis=1)


def column_index(waves):
    g0, flat = waves[:, 0], waves[:, 1] * SIDE + waves[:, 2]
    u = jnp.abs(flat)
    turn = jnp.where(flat < 0, -1, 1)
    side = jnp.sign(g0)
    cos_row = jnp.abs(g0) * LANES + u
    sin_row = jnp.where(g0 == 0, 0, REACH + jnp.abs(g0)) * LANES + u
    half = waves.shape[0] // 2

    def order(cosine, sine):
        return jnp.concatenate([cosine[:half], sine[:half], cosine[half:], sine[half:]])

    return jnp.stack(
        [
            order(cos_row, sin_row),
            order(sin_row + HALF, cos_row + HALF),
            order(jnp.ones_like(g0), side),
            order(-turn * side, turn),
        ]
    )


def vmem(count):
    return [pl.BlockSpec(memory_space=pltpu.VMEM)] * count


SMEM = pl.BlockSpec(memory_space=pltpu.SMEM)


def room(mebibytes):
    return pltpu.CompilerParams(vmem_limit_bytes=mebibytes << 20)


def prepare_kernel(stride, choices, table, energy, empty, occupied, choice, mine, theirs, sent, partner, level, sems):
    half = mine.shape[0]
    points = mine.shape[1]
    core = lax.axis_index("row") % 2
    parts = (core, 1 - core)
    copies = [
        pltpu.make_async_copy(empty.at[0, pl.ds(pl.multiple_of(part * half, half), half)], to, sems.at[i])
        for i, (part, to) in enumerate(zip(parts, (mine, theirs)))
    ]
    copies.append(pltpu.make_async_copy(occupied.at[0], sent.at[:, pl.ds(0, points)], sems.at[2]))
    small = [pltpu.make_async_copy(table, partner, sems.at[3]), pltpu.make_async_copy(energy, level, sems.at[4])]
    for copy in small + copies:
        copy.start()
    for copy in small:
        copy.wait()
    steps = [jnp.clip(partner[moment, 0] // stride, 1, choices) - 1 for moment in range(2)]
    choice[...] = jnp.full(choice.shape, steps[0] * choices + steps[1], jnp.int32)
    states = sent.shape[0]
    square = (states, states)
    here = lax.broadcasted_iota(jnp.int32, square, 0) == lax.broadcasted_iota(jnp.int32, square, 1)
    spread = jnp.where(here, jnp.broadcast_to(level[...].astype(jnp.float32), square), 0.0)
    column = jnp.sum(spread, axis=1, keepdims=True)
    sent[:, points:] = jnp.broadcast_to(column, (states, LANES)).astype(jnp.bfloat16)
    for copy in copies:
        copy.wait()


def prepare(partner, occ_energy, empty, occupied, stride, choices):
    _, bands, points = empty.shape
    states = occupied.shape[1]
    half = jax.ShapeDtypeStruct((bands // 2, points), jnp.bfloat16)
    return pl.pallas_call(
        functools.partial(prepare_kernel, stride, choices),
        out_shape=[
            jax.ShapeDtypeStruct((1, LANES), jnp.int32),
            half,
            half,
            jax.ShapeDtypeStruct((states, points + LANES), jnp.bfloat16),
        ],
        in_specs=[pl.BlockSpec(memory_space=pltpu.HBM)] * 4,
        out_specs=vmem(4),
        scratch_shapes=[
            pltpu.SMEM(partner.shape, partner.dtype),
            pltpu.VMEM(occ_energy.shape, occ_energy.dtype),
            pltpu.SemaphoreType.DMA((5,)),
        ],
        compiler_params=room(4),
        name="prepare",
    )(*[pltpu.with_memory_space_constraint(value, pltpu.HBM) for value in (partner, occ_energy, empty, occupied)])


def settle_kernel(count, *refs):
    for source, to in zip(refs[:count], refs[count:]):
        to[...] = source[...]


def settle(*blocks):
    return pl.pallas_call(
        functools.partial(settle_kernel, len(blocks)),
        out_shape=[pltpu.VMEM(block.shape, block.dtype) for block in blocks],
        in_specs=vmem(len(blocks)),
        out_specs=vmem(len(blocks)),
        compiler_params=room(2),
        name="settle",
    )(*blocks)


def whereabouts():
    r, k = lax.axis_index("row"), lax.axis_index("ka")
    return r % 2, r // 2, k % 2, k // 2


def transform(emp, occ, plane, wide, density, part, after=None):
    bands, points = emp.shape
    states = occ.shape[0]
    sheet = plane.shape[0]
    count = points // sheet
    tile = 16
    if occ.dtype != jnp.float32:
        wide[...] = occ[:, :points].astype(jnp.float32)
        occ = wide

    def fill(v):
        for step in range(count):
            at = slice(step * sheet, (step + 1) * sheet)
            row = jnp.broadcast_to(occ[v : v + 1, at], (tile, sheet)).astype(jnp.bfloat16)
            for top in range(0, bands, tile):
                density[v % 2, step * bands + top : step * bands + top + tile, :] = row * emp[top : top + tile, at]

    fill(0)
    for v in range(states):
        if v + 1 < states:
            fill(v + 1)
        made = jnp.dot(density[v % 2], plane[...], preferred_element_type=jnp.float32)
        made = made[:, :LANES] + made[:, LANES:]
        for step in range(count):
            part[step, v * bands : (v + 1) * bands, :] = made[step * bands : (step + 1) * bands]
        if after is not None and v > 0:
            after(v - 1)
    if after is not None:
        after(states - 1)


def fold_pair(pair, grid_x, near, far, bands, store):
    count = near.shape[0]
    core, x, _, _ = whereabouts()
    lower = core if pair == 0 else 1 - core
    sign = jnp.where(x == 0, jnp.float32(1), jnp.float32(-1))
    middle = (count - 1) / 2
    turn = {}
    for g in range(1, REACH + 1):
        angles = [2.0 * math.pi * g * (row * count + middle) / grid_x for row in range(2)]
        scale = sign if g % 2 else jnp.float32(1)
        turn[g] = [
            jnp.where(lower == 0, jnp.float32(part(angles[0])), jnp.float32(part(angles[1]))) * scale
            for part in (math.cos, math.sin)
        ]
    tall = 8

    def weighted(values, weights):
        total = values[0] * weights[0]
        for value, weight in zip(values[1:], weights[1:]):
            total = total + value * weight
        return total

    def after(v):
        for top in range(v * bands, (v + 1) * bands, tall):
            rows = slice(top, top + tall)
            ones = [near[step, rows, :] for step in range(count)]
            twos = [far[step, rows, :] for step in range(count)]
            for odd in (0, 1):
                both = [one - two if odd else one + two for one, two in zip(ones, twos)]
                half = count // 2
                evens = [both[half + i] + both[half - 1 - i] for i in range(half)]
                odds = [both[half + i] - both[half - 1 - i] for i in range(half)]
                if not odd:
                    store(0, rows, functools.reduce(lambda p, q: p + q, evens))
                for g in range(2 - odd, REACH + 1, 2):
                    angles = [2.0 * math.pi * g * (i + 0.5) / grid_x for i in range(half)]
                    even = weighted(evens, [math.cos(t) for t in angles])
                    rest = weighted(odds, [math.sin(t) for t in angles])
                    c, s = turn[g]
                    store(g, rows, even * c - rest * s)
                    store(REACH + g, rows, even * s + rest * c)

    return after


def first_kernel(emp, occ, plane, part, wide, density):
    transform(emp, occ, plane, wide, density, part)


def own_kernel(emp, occ, plane, energy, part, w_own, w_other, wide, density):
    bands, points = emp.shape
    states = occ.shape[0]
    core = whereabouts()[0]
    shape = (bands, energy.shape[1])
    down = lax.broadcasted_iota(jnp.int32, shape, 0)
    along = lax.broadcasted_iota(jnp.int32, shape, 1)
    levels = jnp.broadcast_to(energy[...].astype(jnp.float32), shape)
    for part_of, weight in ((core, w_own), (1 - core, w_other)):
        column = jnp.sum(jnp.where(along == down + part_of * bands, levels, 0.0), axis=1, keepdims=True)
        column = jnp.broadcast_to(column, (bands, LANES))
        for v in range(states):
            level = occ[v : v + 1, points : points + LANES].astype(jnp.float32)
            weight[v * bands : (v + 1) * bands, :] = 1.0 / (column - level)
    transform(emp, occ, plane, wide, density, part)


def matrix_kernel(index, matrix):
    share = 2 * LANES // 4
    shape = (share, matrix.shape[1])
    signs = index[2:4, :].astype(jnp.float32)

    def body(at, carry):
        start = pl.multiple_of(at * share, share)
        rows = lax.broadcasted_iota(jnp.int32, shape, 0) + start
        two = jnp.where(rows == index[1:2, :], jnp.broadcast_to(signs[1:2], shape), 0.0)
        one = jnp.where(rows == index[0:1, :], jnp.broadcast_to(signs[0:1], shape), two)
        matrix[pl.ds(start, share), :] = one.astype(jnp.bfloat16)
        return carry

    lax.fori_loop(0, matrix.shape[0] // share, body, 0)


def make_matrix(index):
    return pl.pallas_call(
        matrix_kernel,
        out_shape=pltpu.VMEM((FACTORS * LANES, index.shape[1]), jnp.bfloat16),
        in_specs=vmem(1),
        out_specs=vmem(1)[0],
        compiler_params=room(4),
        name="matrix",
    )(index)


def fold_pair(pair, grid_x, near, far, bands, store):
    count = near.shape[0]
    core, x, _, _ = whereabouts()
    lower = core if pair == 0 else 1 - core
    sign = jnp.where(x == 0, jnp.float32(1), jnp.float32(-1))
    middle = (count - 1) / 2
    turn = {}
    for g in range(1, REACH + 1):
        angles = [2.0 * math.pi * g * (row * count + middle) / grid_x for row in range(2)]
        scale = sign if g % 2 else jnp.float32(1)
        turn[g] = [
            jnp.where(lower == 0, jnp.float32(part(angles[0])), jnp.float32(part(angles[1]))) * scale
            for part in (math.cos, math.sin)
        ]
    tall = 8

    def weighted(values, weights):
        total = values[0] * weights[0]
        for value, weight in zip(values[1:], weights[1:]):
            total = total + value * weight
        return total

    def after(v):
        for top in range(v * bands, (v + 1) * bands, tall):
            rows = slice(top, top + tall)
            ones = [near[step, rows, :] for step in range(count)]
            twos = [far[step, rows, :] for step in range(count)]
            for odd in (0, 1):
                both = [one - two if odd else one + two for one, two in zip(ones, twos)]
                half = count // 2
                evens = [both[half + i] + both[half - 1 - i] for i in range(half)]
                odds = [both[half + i] - both[half - 1 - i] for i in range(half)]
                if not odd:
                    store(0, rows, functools.reduce(lambda p, q: p + q, evens))
                for g in range(2 - odd, REACH + 1, 2):
                    angles = [2.0 * math.pi * g * (i + 0.5) / grid_x for i in range(half)]
                    even = weighted(evens, [math.cos(t) for t in angles])
                    rest = weighted(odds, [math.sin(t) for t in angles])
                    c, s = turn[g]
                    store(g, rows, even * c - rest * s)
                    store(REACH + g, rows, even * s + rest * c)

    return after


def first_kernel(emp, occ, plane, part, wide, density):
    transform(emp, occ, plane, wide, density, part)


def middle_pair_kernel(grid_x, emp, occ, plane, near, total, wide, density, part):
    def store(j, rows, value):
        total[j, rows, :] = value

    transform(emp, occ, plane, wide, density, part, fold_pair(0, grid_x, near, part, emp.shape[0], store))


def last_pair_kernel(
    grid_x, scale, emp, occ, plane, near, before, matrix, left, wide, density, part, total, narrow
):
    def store(j, rows, value):
        total[j, rows, :] = before[j, rows, :] + value

    transform(emp, occ, plane, wide, density, part, fold_pair(1, grid_x, near, part, emp.shape[0], store))
    for j in range(FACTORS):
        narrow[:, j * LANES : (j + 1) * LANES] = total[j].astype(jnp.bfloat16)
    proj = jnp.dot(narrow[...], matrix[...], preferred_element_type=jnp.float32)
    left[...] = (proj * scale).astype(jnp.bfloat16)


def scratch_of(emp, states):
    bands, points = emp.shape
    sheet = GY * GZ
    return [
        pltpu.VMEM((states, points), jnp.float32),
        pltpu.VMEM((2, points // sheet * bands, sheet), jnp.bfloat16),
    ]


def project(matrix, blocks, energy, grid_x, scale):
    (own, core, x, far) = blocks
    bands, points = core[0].shape
    states = core[1].shape[0]
    pairs = bands * states
    count = points // (GY * GZ)
    columns = matrix.shape[1]
    plane = jnp.asarray(plane_table())
    part_shape = (count, pairs, LANES)
    total_shape = (FACTORS, pairs, LANES)
    scratch = scratch_of(core[0], states)
    part = pltpu.VMEM(part_shape, jnp.float32)

    def first(kernel, outs, operands):
        return pl.pallas_call(
            kernel,
            out_shape=[jax.ShapeDtypeStruct(shape, jnp.float32) for shape in outs],
            in_specs=vmem(len(operands)),
            out_specs=vmem(len(outs)),
            scratch_shapes=scratch,
            compiler_params=room(6),
        )(*operands)

    weight_shape = (pairs, LANES)
    part_own, w_own, w_other = first(own_kernel, [part_shape] + [weight_shape] * 2, (*own, plane, energy))
    (part_core,) = first(first_kernel, [part_shape], (*core, plane))
    total = pl.pallas_call(
        functools.partial(middle_pair_kernel, grid_x),
        out_shape=jax.ShapeDtypeStruct(total_shape, jnp.float32),
        in_specs=vmem(4),
        out_specs=vmem(1)[0],
        scratch_shapes=scratch + [part],
        compiler_params=room(8),
        name="pair",
    )(*x, plane, part_own)
    left = pl.pallas_call(
        functools.partial(last_pair_kernel, grid_x, scale),
        out_shape=jax.ShapeDtypeStruct((pairs, columns), jnp.bfloat16),
        in_specs=vmem(6),
        out_specs=vmem(1)[0],
        scratch_shapes=scratch
        + [part, pltpu.VMEM(total_shape, jnp.float32), pltpu.VMEM((pairs, FACTORS * LANES), jnp.bfloat16)],
        compiler_params=room(14),
        name="last",
    )(*far, plane, part_core, total, matrix)
    return left, w_own, w_other


def gram_of(core, values, weights):
    width = values.shape[1] // 2
    at = pl.multiple_of(core * width, LANES)
    right = [
        (values[:, pl.ds(at + tile * LANES, LANES)].astype(jnp.float32) * weights[...]).astype(jnp.bfloat16)
        for tile in range(width // LANES)
    ]
    return lax.dot_general(
        values[...], jnp.concatenate(right, axis=1), (((0,), (0,)), ((), ())), preferred_element_type=jnp.float32
    )


def gram_own_kernel(own, w_own, gram):
    gram[...] = gram_of(whereabouts()[0], own, w_own)


def roll_half(value):
    return pltpu.roll(value, value.shape[1] // 2, 1)


def gram_kernel(first, other, w_other, keep, to_y, to_z, to_yz, gram):
    core, _, y, z = whereabouts()
    zl = z % 2
    gram[...] = first[...] + gram_of(core, other, w_other)
    rows = gram.shape[0] // 8
    for out, to_y_of, to_zl in ((keep, y, zl), (to_y, 1 - y, zl), (to_z, y, 1 - zl), (to_yz, 1 - y, 1 - zl)):
        for zh in range(2):
            start = ((2 * to_zl + zh) * 2 + to_y_of) * rows
            out[zh * rows : (zh + 1) * rows, :] = gram[pl.ds(pl.multiple_of(start, 8), rows), :].astype(out.dtype)


def middle_kernel(keep, from_y, from_z, from_yz, stay, to_x, to_z, to_xz, total):
    _, x, _, z = whereabouts()
    zh = z // 2
    rows = keep.shape[0] // 2
    total[...] = (keep[...] + from_y[...].astype(jnp.float32)) + (
        from_z[...].astype(jnp.float32) + from_yz[...].astype(jnp.float32)
    )
    low = lax.broadcasted_iota(jnp.int32, (rows // 2, keep.shape[1]), 1) < keep.shape[1] // 2
    for to_zh, near, far in ((zh, stay, to_x), (1 - zh, to_z, to_xz)):
        top = total[pl.ds(pl.multiple_of(to_zh * rows, 8), rows // 2), :]
        bottom = total[pl.ds(pl.multiple_of(to_zh * rows + rows // 2, 8), rows // 2), :]
        zero = jnp.where(low, top, roll_half(bottom))
        one = jnp.where(low, roll_half(top), bottom)
        near[...] = jnp.where(x == 0, zero, one).astype(near.dtype)
        far[...] = jnp.where(x == 0, one, zero).astype(far.dtype)


def final_kernel(stay, from_x, from_z, from_xz, out):
    x = whereabouts()[1]
    same = stay[...] + from_z[...].astype(jnp.float32)
    cross = from_x[...].astype(jnp.float32) + from_xz[...].astype(jnp.float32)
    rows, width = same.shape[0], same.shape[1] // 2
    for moment in range(2):
        value = jnp.where(x == moment, same, cross)
        out[moment, :rows, :] = value[:, :width]
        out[moment, rows:, :] = roll_half(value)[:, :width]


def reduce_near(own, other, w_own, w_other):
    wide = own.shape[1]
    kcount, rcount = lax.axis_size("ka"), lax.axis_size("row")
    bf16, f32 = jnp.bfloat16, jnp.float32
    first = pl.pallas_call(
        gram_own_kernel,
        out_shape=jax.ShapeDtypeStruct((wide, wide // 2), f32),
        in_specs=vmem(2),
        out_specs=vmem(1)[0],
        compiler_params=room(8),
        name="gram_own",
    )(own, w_own)
    quarter = (wide // 4, wide // 2)
    keep, *sends = pl.pallas_call(
        gram_kernel,
        out_shape=[jax.ShapeDtypeStruct(quarter, d) for d in (f32, bf16, bf16, bf16)],
        in_specs=vmem(3),
        out_specs=vmem(4),
        scratch_shapes=[pltpu.VMEM((wide, wide // 2), f32)],
        compiler_params=room(10),
        name="gram",
    )(first, other, w_other)

    def exchange(values, ways):
        came = []
        for value, (dk, dr) in zip(values, ways):
            pairs = [(k * rcount + r, (k ^ dk) * rcount + (r ^ dr)) for k in range(kcount) for r in range(rcount)]
            came.append(lax.ppermute(value, ("ka", "row"), pairs))
        return came

    came = exchange(sends, ((1, 0), (2, 0), (3, 0)))
    piece = (quarter[0] // 4, quarter[1])
    stay, *sends = pl.pallas_call(
        middle_kernel,
        out_shape=[jax.ShapeDtypeStruct(piece, d) for d in (f32, bf16, bf16, bf16)],
        in_specs=vmem(4),
        out_specs=vmem(4),
        scratch_shapes=[pltpu.VMEM(quarter, f32)],
        compiler_params=room(6),
        name="middle",
    )(keep, *came)
    came = exchange(sends, ((0, 2), (4, 0), (4, 2)))
    return pl.pallas_call(
        final_kernel,
        out_shape=jax.ShapeDtypeStruct((2, piece[0] * 2, piece[1] // 2), f32),
        in_specs=vmem(4),
        out_specs=vmem(1)[0],
        compiler_params=room(4),
        name="final",
    )(stay, *came)


def reduce_far(own, other, w_own, w_other):
    kcount = lax.axis_size("ka")
    core, x, _, _ = whereabouts()
    wide = own.shape[1]
    width = wide // 4
    left = jnp.concatenate([own, other], axis=0)
    weight = jnp.concatenate([w_own[:, :1], w_other[:, :1]], axis=0)
    right = lax.dynamic_slice_in_dim(left, core * 2 * width, 2 * width, 1)
    right = (right.astype(jnp.float32) * weight).astype(jnp.bfloat16)
    gram = lax.dot_general(left, right, (((0,), (0,)), ((), ())), preferred_element_type=jnp.float32)
    gram = gram.reshape(2, 2, width, 2, width).swapaxes(0, 1).reshape(kcount, wide // kcount, 2, width)
    parts = lax.all_to_all(gram.astype(jnp.bfloat16), "ka", 0, 0, tiled=True)
    total = jnp.sum(parts.astype(jnp.float32), axis=0)
    mine = lax.dynamic_index_in_dim(total, x, 1, keepdims=False)
    send = lax.dynamic_index_in_dim(total, 1 - x, 1, keepdims=False)
    came = lax.ppermute(send, "row", [(r, r ^ 2) for r in range(lax.axis_size("row"))])
    first = x == 0
    return jnp.stack([jnp.where(first, mine, came), jnp.where(first, came, mine)])


def per_device(occupied, empty, occ_energy, emp_energy, partner, gvecs):
    kcount, rcount = lax.axis_size("ka"), lax.axis_size("row")
    assert rcount == 4 and partner.shape[0] == 2
    r = lax.axis_index("row")
    x = r // 2
    points = occupied.shape[2]
    grid_x = points * rcount // (GY * GZ)
    stride = kcount // min(SHIFTS, kcount)
    choices = min(SHIFTS, kcount) - 1
    choice, mine, theirs, sent = prepare(partner, occ_energy, empty, occupied, stride, choices)
    emp_x = lax.ppermute(mine, "row", [(i, i ^ 2) for i in range(rcount)])
    emp_xc = lax.ppermute(theirs, "row", [(i, i ^ 3) for i in range(rcount)])
    emp_c = lax.ppermute(theirs, "row", [(i, i ^ 1) for i in range(rcount)])

    swap = [(i, i ^ 1) for i in range(rcount)]

    def fetch(shift, operands):
        block, waves = operands

        def route(dx):
            pairs = []
            for i in range(kcount):
                for j in range(rcount):
                    to = j ^ dx
                    pairs.append((i * rcount + j, (i + shift[to // 2] * stride) % kcount * rcount + to))
            return pairs

        both = ("ka", "row")
        far = lax.ppermute(block, both, route(2))
        near = lax.ppermute(block, both, route(0))
        near_c = lax.ppermute(near, "row", swap)
        matrix = make_matrix(column_index(lax.dynamic_index_in_dim(waves, x, 0, keepdims=False)))
        return *settle(near, near_c, far), matrix

    branches = [functools.partial(fetch, (one + 1, two + 1)) for one in range(choices) for two in range(choices)]
    occ_own, occ_c, occ_x, matrix = lax.switch(choice[0, 0], branches, (sent, gvecs))
    occ_xc = lax.ppermute(occ_x, "row", swap)

    blocks = ((mine, occ_own), (emp_c, occ_c), (emp_x, occ_x), (emp_xc, occ_xc))
    left, w_own, w_other = project(matrix, blocks, emp_energy, grid_x, 1.0 / (points * rcount))
    other = lax.ppermute(left, "row", swap)
    reduce = reduce_near if kcount == 8 else reduce_far
    return reduce(left, other, w_own, w_other)


def solution(mesh):
    placed = (P("ka", None, "row"), P("ka", None, "row"), P("ka", None), P("ka", None), P(), P())

    return jax.shard_map(per_device, mesh=mesh, in_specs=placed, out_specs=P(None, "ka", "row"), check_vma=False)
```
